256 devices in a mesh: row: 32 (over y, z), col: 8 (over x, core).
Axes of the slice: x: 4, y: 4, z: 8, core: 2. Of those that a mesh axis runs over, the one named last changes fastest.
Arguments:
- acts: bfloat16 [6144, 28672], P('col', 'row'), may hold values from -12 to 12
- out_grad: bfloat16 [6144, 8192], P('row', 'col'), may hold values from -12 to 12
- lengths: int32 [8], replicated, may hold values from 1 to 768, 4800 in all
Outputs:
- weight_grad: bfloat16 [28672, 8192], P('row', 'col')
- norms: float32 [8], replicated
The draws below stay inside these ranges and needn't reach their ends.
All inputs are finite; a program needn't handle non-finite values.
Results may differ from the reference program's by a relative error of at most 0.0013.
Values may be sent and summed in bfloat16 or wider, within the bound.
No kernel may reach another device: no remote copies, remote signals or barrier semaphores. Data moves between devices by JAX's collectives and lax.ppermute only.
A program may use at most 128 MiB of HBM per device.

```python
import math
import jax
import jax.numpy as jnp
import numpy as np
from jax import lax

FF = 28672
D = 8192
SEQS = 8
LEN = 768
TOKENS = 6144


shared_count = 8


shared_weight = 0.2


def shared_coeffs(key):
    base = jax.random.fold_in(key, 101)
    scales = jax.random.uniform(jax.random.fold_in(base, 1), (SEQS, shared_count), jnp.float32, 0.4, 1.6)
    coeffs = jax.random.normal(jax.random.fold_in(base, 2), (TOKENS, shared_count), jnp.float32)
    return coeffs * jnp.repeat(scales, LEN, axis=0)


def with_shared(random_part, coeffs, directions):
    total = random_part
    for index in range(shared_count):
        total = total + shared_weight * coeffs[:, index:index + 1] * directions[index][None, :]
    return total


def draw_acts(key, part):
    coeffs = shared_coeffs(key)
    directions = jax.random.normal(jax.random.fold_in(key, 211), (shared_count, FF), jnp.float32)
    random_part = jax.random.normal(jax.random.fold_in(key, 212), (TOKENS, FF), jnp.float32)
    ramp = jnp.arange(FF, dtype=jnp.float32) / jnp.float32(FF - 1)
    rough = jax.random.uniform(jax.random.fold_in(key, 213), (FF,), jnp.float32, 0.7, 1.3)
    feature_scale = jnp.exp(ramp * jnp.log(jnp.float32(3.0))) * rough
    total = with_shared(random_part, coeffs, directions) * feature_scale[None, :]
    return jnp.clip(total, -12.0, 12.0).astype(jnp.bfloat16)


def draw_out_grad(key, part):
    coeffs = shared_coeffs(key)
    directions = jax.random.normal(jax.random.fold_in(key, 311), (shared_count, D), jnp.float32)
    random_part = jax.random.normal(jax.random.fold_in(key, 312), (TOKENS, D), jnp.float32)
    return jnp.clip(with_shared(random_part, coeffs, directions), -12.0, 12.0).astype(jnp.bfloat16)


def length_profile(amount, total, reach, skew):
    weights = [(1 << 20) // math.isqrt(rank ** skew) + 1 for rank in range(2, amount + 1)]
    spare, counts = total - reach - (amount - 1), [1] * (amount - 1)
    while spare > 0:
        candidates = [i for i in range(amount - 1) if counts[i] < reach]
        mass, remaining = sum([weights[i] for i in candidates]), spare
        for i in candidates:
            extra = min(reach - counts[i], max(1, remaining * weights[i] // mass), spare)
            counts[i] = counts[i] + extra
            spare = spare - extra
    return np.array([reach] + counts)


def ragged_sizes(rng, number_of, total, bound, slope):
    if number_of == 2:
        one = jax.random.randint(rng, (), max(1, total - bound), min(bound, total - 1) + 1)
        return jnp.stack([one, total - one])
    sizes = jnp.asarray(length_profile(number_of, total, bound, slope), jnp.int32)
    couples = (number_of - 1) // 2
    giver, receiver = sizes[1:1 + 2 * couples:2], sizes[2:2 + 2 * couples:2]
    slack = jnp.minimum(giver - 1, bound - receiver)
    shifted = jax.random.randint(jax.random.fold_in(rng, 1), (couples,), 0, 1 << 20) % (slack + 1)
    sizes = sizes.at[1:1 + 2 * couples:2].set(giver - shifted).at[2:2 + 2 * couples:2].set(receiver + shifted)
    return sizes[jax.random.permutation(jax.random.fold_in(rng, 2), number_of)]


def setup_inputs(seed: int = 0) -> dict:
    key_list = jax.random.split(jax.random.key(seed), 4)
    acts = draw_acts(jax.random.fold_in(key_list[3], 71), 0)
    out_grad = draw_out_grad(jax.random.fold_in(key_list[3], 71), 0)
    lengths = ragged_sizes(key_list[2], SEQS, SEQS * LEN - (SEQS - 1) * (LEN // 4), LEN, 0).astype(jnp.int32)
    return {"acts": acts, "out_grad": out_grad, "lengths": lengths}


def reference(acts, out_grad, lengths):
    positions = jnp.arange(TOKENS, dtype=jnp.int32)
    seq_of = positions // LEN
    limit = lax.optimization_barrier(jnp.sum(jnp.where(seq_of[:, None] == jnp.arange(SEQS, dtype=jnp.int32)[None, :], lengths[None, :], 0), axis=1))
    live = positions % LEN < limit
    grads = jnp.where(live[:, None], out_grad, jnp.zeros_like(out_grad))
    divisor = float(FF) * float(D) * float(LEN)
    norm_list = []
    for seq in range(SEQS):
        act_rows = acts[seq * LEN:(seq + 1) * LEN]
        grad_rows = grads[seq * LEN:(seq + 1) * LEN]
        act_gram = jnp.dot(act_rows, act_rows.T, preferred_element_type=jnp.float32)
        grad_gram = jnp.dot(grad_rows, grad_rows.T, preferred_element_type=jnp.float32)
        squares = jnp.sum(act_gram * grad_gram)
        norm_list.append(jnp.sqrt(squares / divisor))
    norms = jnp.stack(norm_list).astype(jnp.float32)
    scale = 1.0 / (norms + 0.1)
    total = jnp.zeros((FF, D), jnp.float32)
    for seq in range(SEQS):
        act_rows = acts[seq * LEN:(seq + 1) * LEN]
        grad_rows = grads[seq * LEN:(seq + 1) * LEN]
        total = total + scale[seq] * jnp.dot(act_rows.T, grad_rows, preferred_element_type=jnp.float32)
    weight_grad = (total / jnp.sqrt(jnp.float32(TOKENS))).astype(jnp.bfloat16)
    return (weight_grad, norms)
```

```python
import jax
import jax.numpy as jnp
from jax import lax
from jax.sharding import PartitionSpec as P

FF = 28672
D = 8192


def exchange_sum(value, axis, shifts):
    size = lax.axis_size(axis)
    parts = [value]
    for shift in shifts:
        parts.append(lax.ppermute(value, axis, [(i, i ^ shift) for i in range(size)]))
    while len(parts) > 1:
        parts = [parts[i] + parts[i + 1] for i in range(0, len(parts), 2)]
    return parts[0]


def sum_everywhere(value):
    value = exchange_sum(value, "col", (1,))
    value = exchange_sum(value, "col", (2, 4, 6))
    value = exchange_sum(value, "row", (8, 16, 24))
    value = exchange_sum(value, "row", (1, 2, 3))
    return exchange_sum(value, "row", (4,))


def body(acts, out_grad, lengths):
    n_row = lax.axis_size("row")
    row_idx = lax.axis_index("row")
    own_rows = out_grad.shape[0]
    tokens = own_rows * n_row
    seqs = lengths.shape[0]
    seq_len = tokens // seqs
    positions = row_idx * own_rows + jnp.arange(own_rows, dtype=jnp.int32)
    seq_of = positions // seq_len
    limit = jnp.sum(
        jnp.where(
            seq_of[:, None] == jnp.arange(seqs, dtype=jnp.int32)[None, :], lengths[None, :], 0
        ),
        axis=1,
    )
    live = positions % seq_len < limit
    own_grads = jnp.where(live[:, None], out_grad, jnp.zeros_like(out_grad))
    grads = lax.all_gather(own_grads, "row", axis=0, tiled=True)
    act_full = lax.all_gather(acts, "col", axis=0, tiled=True)
    products = []
    sums = []
    for seq in range(seqs):
        act_rows = act_full[seq * seq_len : (seq + 1) * seq_len]
        grad_rows = grads[seq * seq_len : (seq + 1) * seq_len]
        product = lax.dot_general(
            act_rows, grad_rows, (((0,), (0,)), ((), ())), preferred_element_type=jnp.float32
        )
        products.append(product)
        sums.append(jnp.sum(product * product))
    squares = sum_everywhere(jnp.stack(sums))
    norms = jnp.sqrt(squares / (float(FF) * float(D) * float(seq_len)))
    scale = 1.0 / (norms + 0.1)
    total = scale[0] * products[0]
    for seq in range(1, seqs):
        total = total + scale[seq] * products[seq]
    weight_grad = (total / jnp.sqrt(jnp.float32(tokens))).astype(jnp.bfloat16)
    return (weight_grad, norms)


def solution(mesh):
    placed = (P("col", "row"), P("row", "col"), P())
    return jax.shard_map(
        body, mesh=mesh, in_specs=placed, out_specs=(P("row", "col"), P()), check_vma=False
    )
```
